32 devices in a mesh: layer: 4 (over x, core), row: 4 (over z), col: 2 (over y).
Axes of the slice: x: 2, y: 2, z: 4, core: 2. Of those that a mesh axis runs over, the one named last changes fastest.
Arguments:
- sources: bfloat16 [4, 96, 12288], P('layer', 'col', 'row'), may hold values from -6 to 6
- transmission: bfloat16 [4, 12288, 12288], P('layer', 'row', 'col'), may hold values from -0.0546875 to 0.0546875
- reflection: bfloat16 [4, 12288, 12288], P('layer', 'row', 'col'), may hold values from -0.02734375 to 0.02734375
Outputs:
- upgoing: bfloat16 [4, 96, 12288], P('layer', 'col', 'row')
The draws below stay inside these ranges and needn't reach their ends.
All inputs are finite; a program needn't handle non-finite values.
Results may differ from the reference program's by a relative error of at most 0.012.
Values may be sent and summed in bfloat16 or wider, within the bound.
A program may use at most 128 MiB of HBM per device.

```python
import jax
import jax.numpy as jnp
from jax import lax

M = 12288
TRACES = 96
LAYERS = 4


def block_levels(own_key, dims, shards, smallest, high):
    gain, own = 1.0, jax.random.fold_in(own_key, 6)
    for position, shards_of in shards:
        steps = jnp.exp(jax.random.uniform(jax.random.fold_in(own, position), (shards_of,), jnp.float32, smallest / len(shards), high / len(shards)))
        gain = gain * jnp.repeat(steps, dims[position] // shards_of).reshape([-1 if axis == position else 1 for axis in range(len(dims))])
    return gain


def normal_values(rng, dims, spread, limit, shards=(), dtype=jnp.bfloat16):
    gain = block_levels(rng, dims, shards, -0.22, 0.18) if shards else 1.0
    entries = jax.random.normal(rng, dims, jnp.float32) * spread * gain
    return jnp.minimum(jnp.maximum(entries, -limit), limit).astype(dtype)


def setup_inputs(seed: int = 0) -> dict:
    key_of = jax.random.split(jax.random.key(seed), 4)
    sources = normal_values(key_of[0], (LAYERS, TRACES, M), 1.0, 6.0, ((0, 4), (1, 2), (2, 4)))
    transmission = normal_values(key_of[1], (LAYERS, M, M), M ** -0.5, 0.0546875, ((0, 4), (1, 4), (2, 2)))
    reflection = normal_values(key_of[2], (LAYERS, M, M), (4 * M) ** -0.5, 0.02734375, ((0, 4), (1, 4), (2, 2)))
    return {"sources": sources, "transmission": transmission, "reflection": reflection}


def reference(sources, transmission, reflection):
    down = jnp.zeros((TRACES, M), jnp.bfloat16)
    incidents = []
    for level in range(LAYERS):
        incident = (down.astype(jnp.float32) + sources[level].astype(jnp.float32)).astype(jnp.bfloat16)
        incidents.append(incident)
        down = jnp.dot(incident, transmission[level], preferred_element_type=jnp.float32).astype(jnp.bfloat16)
    upward = down
    results = [None] * LAYERS
    for level in reversed(range(LAYERS)):
        passed = lax.dot_general(upward, transmission[level], (((1,), (1,)), ((), ())), preferred_element_type=jnp.float32)
        bounced = lax.dot_general(incidents[level], reflection[level], (((1,), (1,)), ((), ())), preferred_element_type=jnp.float32)
        upward = (passed + bounced).astype(jnp.bfloat16)
        results[level] = upward
    return jnp.stack(results)
```

```python
import functools

import jax
import jax.numpy as jnp
from jax import lax
from jax.experimental import pallas as pl
from jax.experimental.pallas import tpu as pltpu
from jax.sharding import PartitionSpec as P

MESH = pl.DeviceIdType.MESH
BF16 = jnp.bfloat16
F32 = jnp.float32


def kernel(
    layers, rows, cols, pieces, r_tile,
    src_ref, trans_ref, refl_ref, out_ref,
    tv, rbuf, sall, nin, incn, pbuf, ybuf, zbuf, nat, ginc, gup, acc, ubuf, urec, upnat,
    t_sem, r_sem, s_send, s_recv, n_send, n_recv, y_send, y_recv, z_send, z_recv,
    g1_send, g1_recv, g2_send, g2_recv, u_send, u_recv, v_send, v_recv,
):
    ratio = rows // cols
    chunks = ratio * pieces
    lay, row, col = (lax.axis_index(name) for name in ("layer", "row", "col"))
    part, cw = nat.shape[1], nat.shape[2]
    traces = cols * part
    r_count = refl_ref.shape[0] // r_tile
    last = layers - 1

    def other(index, by, size):
        return lax.rem(index + by, size)

    def remote(src, dst, send, recv, target):
        return pltpu.make_async_remote_copy(
            src_ref=src, dst_ref=dst, send_sem=send, recv_sem=recv,
            device_id=target, device_id_type=MESH,
        )

    def t_copy(j):
        start = pl.multiple_of(j * cw, 128)
        return pltpu.make_async_copy(trans_ref.at[:, pl.ds(start, cw)], tv.at[j], t_sem.at[j])

    def r_copy(i, slot):
        start = pl.multiple_of(i * r_tile, 16)
        return pltpu.make_async_copy(
            refl_ref.at[pl.ds(start, r_tile), :], rbuf.at[slot], r_sem.at[slot]
        )

    def copy_src(c):
        return remote(src_ref, sall.at[col], s_send.at[c], s_recv.at[col], (lay, row, c))

    def got_src(c):
        return remote(src_ref, sall.at[c], s_send.at[c], s_recv.at[c], (lay, row, c))

    def copy_next(c, p):
        return remote(nat.at[p], nin.at[col, p], n_send.at[c, p], n_recv.at[col, p],
                      (lax.min(lay + 1, last), row, c))

    def got_next(c, p):
        return remote(nat.at[p], nin.at[c, p], n_send.at[c, p], n_recv.at[c, p],
                      (lax.max(lay - 1, 0), row, c))

    def copy_y(c, j):
        return remote(pbuf.at[j, c], ybuf.at[col, j], y_send.at[c, j], y_recv.at[col, j],
                      (lay, row, c))

    def got_y(c, j):
        return remote(pbuf.at[j, c], ybuf.at[c, j], y_send.at[c, j], y_recv.at[c, j],
                      (lay, row, c))

    def copy_z(c, j, own):
        block = pbuf.at[j, col] if own else ybuf.at[c, j]
        goal = ratio * c + lax.div(j, pieces)
        return goal, block, remote(
            block, zbuf.at[row, lax.rem(j, pieces)], z_send.at[c, j],
            z_recv.at[row, lax.rem(j, pieces)], (lay, goal, col),
        )

    def got_z(r, p):
        return remote(nat.at[p], zbuf.at[r, p], z_send.at[0, 0], z_recv.at[r, p],
                      (lay, r, col))

    def copy_g1(which, buf, r):
        return remote(buf.at[row, :, col], buf.at[row, :, col], g1_send.at[which, r],
                      g1_recv.at[which, row], (lay, r, col))

    def got_g1(which, buf, r):
        return remote(buf.at[r, :, col], buf.at[r, :, col], g1_send.at[which, r],
                      g1_recv.at[which, r], (lay, r, col))

    def copy_g2(which, buf, r):
        return remote(buf.at[r, :, col], buf.at[r, :, col], g2_send.at[which, r],
                      g2_recv.at[which, r, col], (lay, row, lax.div(r, ratio)))

    def got_g2(which, buf, r, c):
        return remote(buf.at[r, :, c], buf.at[r, :, c], g2_send.at[which, r],
                      g2_recv.at[which, r, c], (lay, row, c))

    def copy_u(c):
        return remote(ubuf.at[c], urec.at[col], u_send.at[c], u_recv.at[col], (lay, row, c))

    def got_u(c):
        return remote(ubuf.at[c], urec.at[c], u_send.at[c], u_recv.at[c], (lay, row, c))

    def copy_v():
        return remote(nat, upnat, v_send, v_recv, (lax.max(lay - 1, 0), row, col))

    def got_v():
        return remote(nat, upnat, v_send, v_recv, (lax.min(lay + 1, last), row, col))

    for j in range(chunks):
        t_copy(j).start()

    barrier = pltpu.get_barrier_semaphore()

    def greet(target):
        pl.semaphore_signal(barrier, inc=1, device_id=target, device_id_type=MESH)

    for d in range(1, rows):
        greet((lay, other(row, d, rows), col))
    for d in range(1, cols):
        greet((lay, row, other(col, d, cols)))

    @pl.when(lay > 0)
    def _():
        for c in range(cols):
            greet((lay - 1, row, c))

    @pl.when(lay < last)
    def _():
        for c in range(cols):
            greet((lay + 1, row, c))

    near = (lay > 0).astype(jnp.int32) + (lay < last).astype(jnp.int32)
    pl.semaphore_wait(barrier, rows + cols - 2 + cols * near)

    for d in range(1, cols):
        copy_src(other(col, d, cols)).start()
    sall[col] = src_ref[...]
    for d in range(1, cols):
        got_src(other(col, d, cols)).wait_recv()

    @pl.when(lay == 0)
    def _():
        for p in range(pieces):
            incn[p] = sall[:, p]

    @pl.when(lay > 0)
    def _():
        for p in range(pieces):
            for c in range(cols):
                got_next(c, p).wait_recv()
            incn[p] = (nin[:, p].astype(F32) + sall[:, p].astype(F32)).astype(BF16)

    for p in range(pieces):
        ginc[row, p, col] = incn[p, col]
    for d in range(1, rows):
        copy_g1(0, ginc, other(row, d, rows)).start()

    def to_row(c, j, own):
        goal, block, copy = copy_z(c, j, own)

        @pl.when(goal == row)
        def _():
            zbuf[row, lax.rem(j, pieces)] = block[...]

        @pl.when(goal != row)
        def _():
            copy.start()

    def forward(j):
        for d in range(1, cols):
            c = other(col, d, cols)
            got_y(c, j).wait_recv()
            to_row(c, j, False)

    def down_step(j, carry):
        t_copy(j).wait()
        total = jnp.zeros((traces, cw), F32)
        for p in range(pieces):
            total += jnp.dot(
                incn[p].reshape(traces, cw), tv[j, pl.ds(p * cw, cw), :],
                preferred_element_type=F32,
            )
        pbuf[j] = total.astype(BF16).reshape(cols, part, cw)
        for d in range(1, cols):
            copy_y(other(col, d, cols), j).start()
        to_row(col, j, True)

        @pl.when(j > 0)
        def _():
            forward(j - 1)

        return carry

    lax.fori_loop(0, chunks, down_step, 0)
    forward(chunks - 1)

    for p in range(pieces):
        for d in range(1, rows):
            got_z(other(row, d, rows), p).wait_recv()
        nat[p] = jnp.sum(zbuf[:, p].astype(F32), axis=0).astype(BF16)

        @pl.when(lay < last)
        def _():
            for c in range(cols):
                copy_next(c, p).start()

    def set_out(block):
        gup[row, :, col] = block[...]
        for d in range(1, rows):
            copy_g1(1, gup, other(row, d, rows)).start()

    @pl.when(lay == last)
    def _():
        set_out(nat)

    def spread(which, buf):
        for d in range(rows):
            r = other(row, d, rows)
            if d > 0:
                got_g1(which, buf, r).wait_recv()

            @pl.when(lax.div(r, ratio) != col)
            def _():
                copy_g2(which, buf, r).start()

    def complete(which, buf, b):
        for d in range(1, cols):
            got_g2(which, buf, ratio * col + b, other(col, d, cols)).wait_recv()

    contract = (((1,), (1,)), ((), ()))

    r_copy(0, 0).start()
    spread(0, ginc)
    for b in range(ratio):
        complete(0, ginc, b)

    def reflect_step(i, carry):
        slot = lax.rem(i, 2)
        r_copy(i, slot).wait()

        @pl.when(i + 1 < r_count)
        def _():
            r_copy(i + 1, 1 - slot).start()

        total = jnp.zeros((traces, r_tile), F32)
        for b in range(ratio):
            for p in range(pieces):
                total += lax.dot_general(
                    ginc[ratio * col + b, p].reshape(traces, cw),
                    rbuf[slot, :, pl.ds((b * pieces + p) * cw, cw)],
                    contract, preferred_element_type=F32,
                )
        acc[i] = total
        return carry

    lax.fori_loop(0, r_count, reflect_step, 0)

    @pl.when(lay < last)
    def _():
        got_v().wait_recv()
        set_out(upnat)

    spread(1, gup)

    def up_step(j, carry):
        lhs = gup[ratio * col + lax.div(j, pieces), lax.rem(j, pieces)].reshape(traces, cw)
        for i in range(r_count):
            acc[i] += lax.dot_general(
                lhs, tv[j, pl.ds(i * r_tile, r_tile), :], contract, preferred_element_type=F32
            )
        return carry

    for b in range(ratio):
        complete(1, gup, b)
        lax.fori_loop(b * pieces, (b + 1) * pieces, up_step, 0)

    per = cw // r_tile

    def piece_of(p, c):
        tiles = []
        for i in range(per):
            tiles.append(acc[p * per + i, pl.ds(pl.multiple_of(c * part, 8), part), :])
        return jnp.concatenate(tiles, axis=1)

    for d in range(1, cols):
        c = other(col, d, cols)
        for p in range(pieces):
            ubuf[c, p] = piece_of(p, c).astype(BF16)
        copy_u(c).start()

    @pl.when(lay < last)
    def _():
        for c in range(cols):
            for p in range(pieces):
                copy_next(c, p).wait_send()

    for d in range(1, cols):
        got_u(other(col, d, cols)).wait_recv()
    for p in range(pieces):
        total = piece_of(p, col)
        for d in range(1, cols):
            total += urec[other(col, d, cols), p].astype(F32)
        result = total.astype(BF16)
        nat[p] = result
        out_ref[:, p * cw:(p + 1) * cw] = result

    @pl.when(lay > 0)
    def _():
        copy_v().start()

    for d in range(1, cols):
        c = other(col, d, cols)
        copy_src(c).wait_send()
        copy_u(c).wait_send()
        for j in range(chunks):
            copy_y(c, j).wait_send()
    for d in range(cols):
        c = other(col, d, cols)
        for j in range(chunks):
            goal, _, copy = copy_z(c, j, d == 0)

            @pl.when(goal != row)
            def _():
                copy.wait_send()

    for which, buf in ((0, ginc), (1, gup)):
        for d in range(1, rows):
            copy_g1(which, buf, other(row, d, rows)).wait_send()
        for r in range(rows):
            @pl.when(r // ratio != col)
            def _():
                copy_g2(which, buf, r).wait_send()

    @pl.when(lay > 0)
    def _():
        copy_v().wait_send()


def split_of(width):
    for pieces in (4, 3, 2):
        if width % (pieces * 128) == 0:
            return pieces
    return 1


def per_device(layers, rows, cols, sources, transmission, reflection):
    ratio = rows // cols
    own, width = sources.shape[1], sources.shape[2]
    part = -(-own // 16) * 16
    pieces = split_of(width)
    cw = width // pieces
    chunks = ratio * pieces
    r_tile = 256 if cw % 256 == 0 else 128
    traces = cols * part
    src = jnp.pad(sources[0], ((0, part - own), (0, 0)))
    src = src.reshape(part, pieces, cw).transpose(1, 0, 2)
    dma, vmem = pltpu.SemaphoreType.DMA, pltpu.VMEM
    result = pl.pallas_call(
        functools.partial(kernel, layers, rows, cols, pieces, r_tile),
        out_shape=jax.ShapeDtypeStruct((part, width), BF16),
        in_specs=[
            pl.BlockSpec(memory_space=pltpu.VMEM),
            pl.BlockSpec(memory_space=pl.ANY),
            pl.BlockSpec(memory_space=pl.ANY),
        ],
        out_specs=pl.BlockSpec(memory_space=pltpu.VMEM),
        scratch_shapes=[
            vmem((chunks, width, cw), BF16),
            vmem((2, r_tile, ratio * width), BF16),
            vmem((cols, pieces, part, cw), BF16),
            vmem((cols, pieces, part, cw), BF16),
            vmem((pieces, cols, part, cw), BF16),
            vmem((chunks, cols, part, cw), BF16),
            vmem((cols, chunks, part, cw), BF16),
            vmem((rows, pieces, part, cw), BF16),
            vmem((pieces, part, cw), BF16),
            vmem((rows, pieces, cols, part, cw), BF16),
            vmem((rows, pieces, cols, part, cw), BF16),
            vmem((width // r_tile, traces, r_tile), F32),
            vmem((cols, pieces, part, cw), BF16),
            vmem((cols, pieces, part, cw), BF16),
            vmem((pieces, part, cw), BF16),
            dma((chunks,)), dma((2,)),
            dma((cols,)), dma((cols,)),
            dma((cols, pieces)), dma((cols, pieces)),
            dma((cols, chunks)), dma((cols, chunks)),
            dma((cols, chunks)), dma((rows, pieces)),
            dma((2, rows)), dma((2, rows)),
            dma((2, rows)), dma((2, rows, cols)),
            dma((cols,)), dma((cols,)),
            dma, dma,
        ],
        compiler_params=pltpu.CompilerParams(
            collective_id=0, has_side_effects=True, vmem_limit_bytes=66_000_000
        ),
    )(src, transmission[0], reflection[0])
    return result[None, :own]


def solution(mesh):
    sizes = [mesh.shape[name] for name in ("layer", "row", "col")]
    return jax.shard_map(
        functools.partial(per_device, *sizes),
        mesh=mesh,
        in_specs=(P("layer", "col", "row"), P("layer", "row", "col"), P("layer", "row", "col")),
        out_specs=P("layer", "col", "row"),
        check_vma=False,
    )
```

```python
import functools

import jax
import jax.numpy as jnp
from jax import lax
from jax.experimental import pallas as pl
from jax.experimental.pallas import tpu as pltpu
from jax.sharding import PartitionSpec as P

MESH = pl.DeviceIdType.MESH
BF16 = jnp.bfloat16
F32 = jnp.float32


def kernel(
    layers, rows, cols, pieces, r_tile,
    src_ref, trans_ref, refl_ref, out_ref,
    tv, rbuf, sall, nin, incn, pbuf, ybuf, zbuf, natd, natu, ginc, gup, acc, ubuf, urec,
    t_sem, r_sem, s_send, s_recv, n_send, n_recv, y_send, y_recv, z_send, z_recv,
    g_send, g_recv, u_send, u_recv, go_sem,
):
    ratio = rows // cols
    chunks = ratio * pieces
    lay, row, col = (lax.axis_index(name) for name in ("layer", "row", "col"))
    part, cw = natd.shape[1], natd.shape[2]
    traces = cols * part
    tiles = acc.shape[0]
    last = layers - 1
    home_col, home_b = lax.div(row, ratio), lax.rem(row, ratio)

    def other(index, by, size):
        return lax.rem(index + by, size)

    def remote(src, dst, send, recv, target):
        return pltpu.make_async_remote_copy(
            src_ref=src, dst_ref=dst, send_sem=send, recv_sem=recv,
            device_id=target, device_id_type=MESH,
        )

    def column_block(step):
        return lax.rem(step, ratio) * pieces + lax.div(step, ratio)

    def t_copy(j):
        start = pl.multiple_of(j * cw, 128)
        return pltpu.make_async_copy(trans_ref.at[:, pl.ds(start, cw)], tv.at[j], t_sem.at[j])

    def r_copy(step):
        start = pl.multiple_of(column_block(step) * cw, 128)
        slot = lax.rem(step, 2)
        return pltpu.make_async_copy(
            refl_ref.at[:, pl.ds(start, cw)], rbuf.at[slot], r_sem.at[slot]
        )

    def copy_src(c):
        return remote(sall.at[col], sall.at[col], s_send.at[c], s_recv.at[col], (lay, row, c))

    def got_src(c):
        return remote(sall.at[c], sall.at[c], s_send.at[c], s_recv.at[c], (lay, row, c))

    def copy_next(c, p):
        return remote(natd.at[p], nin.at[col, p], n_send.at[c, p], n_recv.at[col, p],
                      (lax.min(lay + 1, last), row, c))

    def got_next(c, p):
        return remote(natd.at[p], nin.at[c, p], n_send.at[c, p], n_recv.at[c, p],
                      (lax.max(lay - 1, 0), row, c))

    def copy_y(c, j):
        return remote(pbuf.at[j, c], ybuf.at[col, j], y_send.at[c, j], y_recv.at[col, j],
                      (lay, row, c))

    def got_y(c, j):
        return remote(pbuf.at[j, c], ybuf.at[c, j], y_send.at[c, j], y_recv.at[c, j],
                      (lay, row, c))

    def copy_z(c, j, own):
        block = pbuf.at[j, col] if own else ybuf.at[c, j]
        goal = ratio * c + lax.div(j, pieces)
        return goal, block, remote(
            block, zbuf.at[row, lax.rem(j, pieces)], z_send.at[c, j],
            z_recv.at[row, lax.rem(j, pieces)], (lay, goal, col),
        )

    def got_z(r, p):
        return remote(natd.at[p], zbuf.at[r, p], z_send.at[0, 0], z_recv.at[r, p],
                      (lay, r, col))

    def copy_g(which, p, r):
        block = incn.at[p, col] if which == 0 else (natd, natu)[which - 1].at[p]
        buf, slot = (ginc, 0) if which == 0 else (gup, 1)
        target = lax.max(lay - 1, 0) if which == 2 else lay
        return block, buf, remote(
            block, buf.at[home_b, p, col], g_send.at[which, p, r],
            g_recv.at[slot, p, home_b, col], (target, r, home_col),
        )

    def got_g(slot, p, b, c):
        buf = gup if slot else ginc
        return remote(natd.at[p], buf.at[b, p, c], g_send.at[0, 0, 0],
                      g_recv.at[slot, p, b, c], (lay, ratio * col + b, c))

    def send_g(which, p):
        for d in range(1, rows):
            copy_g(which, p, other(row, d, rows))[2].start()
        block, buf, copy = copy_g(which, p, row)
        if which == 2:
            copy.start()
            return

        @pl.when(home_col == col)
        def _():
            buf[home_b, p, col] = block[...]

        @pl.when(home_col != col)
        def _():
            copy.start()

    def sent_g(which, p):
        for d in range(1, rows):
            copy_g(which, p, other(row, d, rows))[2].wait_send()
        copy = copy_g(which, p, row)[2]
        if which == 2:
            copy.wait_send()
            return

        @pl.when(home_col != col)
        def _():
            copy.wait_send()

    def arrived_g(slot, p, b):
        for c in range(cols):
            mine = (ratio * col + b == row) & (col == c)
            if slot:
                mine = mine & (lay == last)

            @pl.when(jnp.logical_not(mine))
            def _():
                got_g(slot, p, b, c).wait_recv()

    def copy_u(c, p):
        return remote(ubuf.at[c, p], urec.at[col, p], u_send.at[c, p], u_recv.at[col, p],
                      (lay, row, c))

    def got_u(c, p):
        return remote(ubuf.at[c, p], urec.at[c, p], u_send.at[c, p], u_recv.at[c, p],
                      (lay, row, c))

    for step in range(chunks):
        t_copy((step % ratio) * pieces + step // ratio).start()

    barrier = pltpu.get_barrier_semaphore()

    def greet(target):
        pl.semaphore_signal(barrier, inc=1, device_id=target, device_id_type=MESH)

    for dr in range(rows):
        for dc in range(cols):
            if dr or dc:
                greet((lay, other(row, dr, rows), other(col, dc, cols)))

    @pl.when(lay > 0)
    def _():
        for r in range(rows):
            for c in range(cols):
                greet((lay - 1, r, c))

    @pl.when(lay < last)
    def _():
        for r in range(rows):
            for c in range(cols):
                greet((lay + 1, r, c))

    near = (lay > 0).astype(jnp.int32) + (lay < last).astype(jnp.int32)
    pl.semaphore_wait(barrier, rows * cols - 1 + rows * cols * near)

    for p in range(pieces):
        sall[col, p] = src_ref[:, p * cw:(p + 1) * cw]
    for d in range(1, cols):
        copy_src(other(col, d, cols)).start()
    for step in range(2):
        r_copy(step).start()
    acc[...] = jnp.zeros_like(acc)
    for d in range(1, cols):
        got_src(other(col, d, cols)).wait_recv()

    @pl.when(lay == 0)
    def _():
        for p in range(pieces):
            incn[p] = sall[:, p]

    @pl.when(lay > 0)
    def _():
        for p in range(pieces):
            for c in range(cols):
                got_next(c, p).wait_recv()
            incn[p] = (nin[:, p].astype(F32) + sall[:, p].astype(F32)).astype(BF16)

    def to_row(c, j, own):
        goal, block, copy = copy_z(c, j, own)

        @pl.when(goal == row)
        def _():
            zbuf[row, lax.rem(j, pieces)] = block[...]

        @pl.when(goal != row)
        def _():
            copy.start()

    def forward(j):
        for d in range(1, cols):
            c = other(col, d, cols)
            got_y(c, j).wait_recv()
            to_row(c, j, False)

    def down_step(step, carry):
        j = column_block(step)
        t_copy(j).wait()
        total = jnp.zeros((traces, cw), F32)
        for p in range(pieces):
            total += jnp.dot(
                incn[p].reshape(traces, cw), tv[j, pl.ds(p * cw, cw), :],
                preferred_element_type=F32,
            )
        pbuf[j] = total.astype(BF16).reshape(cols, part, cw)
        for d in range(1, cols):
            copy_y(other(col, d, cols), j).start()
        to_row(col, j, True)

        @pl.when(step > 0)
        def _():
            forward(column_block(step - 1))

        return carry

    lax.fori_loop(0, chunks, down_step, 0)
    forward(column_block(chunks - 1))

    @pl.when(lay == last)
    def _():
        for p in range(pieces):
            send_g(0, p)

    for p in range(pieces):
        for d in range(1, rows):
            got_z(other(row, d, rows), p).wait_recv()
        natd[p] = jnp.sum(zbuf[:, p].astype(F32), axis=0).astype(BF16)

        @pl.when(lay < last)
        def _():
            for c in range(cols):
                copy_next(c, p).start()

        @pl.when(lay == last)
        def _():
            send_g(1, p)

    def signal_go():
        pl.semaphore_signal(
            go_sem, inc=1, device_id=(lay - 1, row, col), device_id_type=MESH
        )

    @pl.when((lay > 0) & (lay < last))
    def _():
        signal_go()

    @pl.when(lay < last)
    def _():
        early = pieces // 2
        for p in range(early):
            send_g(0, p)
        pl.semaphore_wait(go_sem, 1)
        for p in range(early, pieces):
            send_g(0, p)

    contract = (((1,), (1,)), ((), ()))

    def times(lhs, rhs):
        return lax.dot_general(lhs, rhs, contract, preferred_element_type=F32)

    def add_product(lhs, weights):
        for i in range(tiles):
            acc[i] += times(lhs, weights[pl.ds(i * r_tile, r_tile), :])

    def reflect_step(step, carry):
        b, p = lax.rem(step, ratio), lax.div(step, ratio)
        arrived_g(0, p, b)
        r_copy(step).wait()
        add_product(ginc[b, p].reshape(traces, cw), rbuf.at[lax.rem(step, 2)])

        @pl.when(step + 2 < chunks)
        def _():
            r_copy(step + 2).start()

        return carry

    lax.fori_loop(0, chunks, reflect_step, 0)

    def up_step(step, carry):
        b, p = lax.rem(step, ratio), lax.div(step, ratio)
        arrived_g(1, p, b)
        add_product(gup[b, p].reshape(traces, cw), tv.at[b * pieces + p])
        return carry

    lax.fori_loop(0, chunks - ratio, up_step, 0)
    end = pieces - 1
    for b in range(ratio):
        arrived_g(1, end, b)

    @pl.when((lay > 0) & (lay == last))
    def _():
        signal_go()

    per = cw // r_tile

    def piece_of(p, c):
        found = []
        for i in range(per):
            found.append(acc[p * per + i, pl.ds(pl.multiple_of(c * part, 8), part), :])
        return jnp.concatenate(found, axis=1)

    for p in range(pieces):
        for i in range(p * per, (p + 1) * per):
            total = acc[i]
            for b in range(ratio):
                total += times(
                    gup[b, end].reshape(traces, cw),
                    tv[b * pieces + end, pl.ds(i * r_tile, r_tile), :],
                )
            acc[i] = total
        for d in range(1, cols):
            c = other(col, d, cols)
            ubuf[c, p] = piece_of(p, c).astype(BF16)
            copy_u(c, p).start()

    for p in range(pieces):
        total = piece_of(p, col)
        for d in range(1, cols):
            c = other(col, d, cols)
            got_u(c, p).wait_recv()
            total += urec[c, p].astype(F32)
        result = total.astype(BF16)
        natu[p] = result
        out_ref[:, p * cw:(p + 1) * cw] = result

        @pl.when(lay > 0)
        def _():
            send_g(2, p)

    for d in range(1, cols):
        c = other(col, d, cols)
        copy_src(c).wait_send()
        for p in range(pieces):
            copy_u(c, p).wait_send()
        for j in range(chunks):
            copy_y(c, j).wait_send()
    for d in range(cols):
        c = other(col, d, cols)
        for j in range(chunks):
            goal, _, copy = copy_z(c, j, d == 0)

            @pl.when(goal != row)
            def _():
                copy.wait_send()

    for p in range(pieces):
        sent_g(0, p)

        @pl.when(lay < last)
        def _():
            for c in range(cols):
                copy_next(c, p).wait_send()

        @pl.when(lay == last)
        def _():
            sent_g(1, p)

        @pl.when(lay > 0)
        def _():
            sent_g(2, p)


def split_of(width):
    for pieces in (4, 3, 2):
        if width % (pieces * 128) == 0:
            return pieces
    return 1


def per_device(layers, rows, cols, sources, transmission, reflection):
    ratio = rows // cols
    own, width = sources.shape[1], sources.shape[2]
    part = -(-own // 16) * 16
    pieces = split_of(width)
    cw = width // pieces
    chunks = ratio * pieces
    r_tile = 256 if cw % 256 == 0 else 128
    traces = cols * part
    src = jnp.pad(sources[0], ((0, part - own), (0, 0)))
    dma, vmem = pltpu.SemaphoreType.DMA, pltpu.VMEM
    result = pl.pallas_call(
        functools.partial(kernel, layers, rows, cols, pieces, r_tile),
        out_shape=jax.ShapeDtypeStruct((part, width), BF16),
        in_specs=[
            pl.BlockSpec(memory_space=pltpu.VMEM),
            pl.BlockSpec(memory_space=pl.ANY),
            pl.BlockSpec(memory_space=pl.ANY),
        ],
        out_specs=pl.BlockSpec(memory_space=pltpu.VMEM),
        scratch_shapes=[
            vmem((chunks, width, cw), BF16),
            vmem((2, width, cw), BF16),
            vmem((cols, pieces, part, cw), BF16),
            vmem((cols, pieces, part, cw), BF16),
            vmem((pieces, cols, part, cw), BF16),
            vmem((chunks, cols, part, cw), BF16),
            vmem((cols, chunks, part, cw), BF16),
            vmem((rows, pieces, part, cw), BF16),
            vmem((pieces, part, cw), BF16),
            vmem((pieces, part, cw), BF16),
            vmem((ratio, pieces, cols, part, cw), BF16),
            vmem((ratio, pieces, cols, part, cw), BF16),
            vmem((width // r_tile, traces, r_tile), F32),
            vmem((cols, pieces, part, cw), BF16),
            vmem((cols, pieces, part, cw), BF16),
            dma((chunks,)), dma((2,)),
            dma((cols,)), dma((cols,)),
            dma((cols, pieces)), dma((cols, pieces)),
            dma((cols, chunks)), dma((cols, chunks)),
            dma((cols, chunks)), dma((rows, pieces)),
            dma((3, pieces, rows)), dma((2, pieces, ratio, cols)),
            dma((cols, pieces)), dma((cols, pieces)),
            pltpu.SemaphoreType.REGULAR,
        ],
        compiler_params=pltpu.CompilerParams(
            collective_id=0, has_side_effects=True, vmem_limit_bytes=66_000_000
        ),
    )(src, transmission[0], reflection[0])
    return result[None, :own]


def solution(mesh):
    sizes = [mesh.shape[name] for name in ("layer", "row", "col")]
    return jax.shard_map(
        functools.partial(per_device, *sizes),
        mesh=mesh,
        in_specs=(P("layer", "col", "row"), P("layer", "row", "col"), P("layer", "row", "col")),
        out_specs=P("layer", "col", "row"),
        check_vma=False,
    )
```

```python
import functools

import jax
import jax.numpy as jnp
from jax import lax
from jax.experimental import pallas as pl
from jax.experimental.pallas import tpu as pltpu
from jax.sharding import PartitionSpec as P

MESH = pl.DeviceIdType.MESH
BF16 = jnp.bfloat16
F32 = jnp.float32


def kernel(
    layers, rows, cols, pieces, r_tile,
    src_ref, trans_ref, refl_ref, out_ref,
    tv, rbuf, sall, nin, incn, pbuf, ybuf, zbuf, natd, natu, lent, ginc, gup, acc, ubuf, urec,
    t_sem, r_sem, s_send, s_recv, n_send, n_recv, y_send, y_recv, z_send, z_recv,
    g_send, g_recv, u_send, u_recv, l_send, l_recv,
):
    ratio = rows // cols
    chunks = ratio * pieces
    lay, row, col = (lax.axis_index(name) for name in ("layer", "row", "col"))
    part, cw = natd.shape[1], natd.shape[2]
    traces = cols * part
    tiles = acc.shape[0]
    last = layers - 1
    half = layers // 2
    helper = lax.rem(lay + half, layers)
    helped = lax.rem(lay + layers - half, layers)
    home_col, home_b = lax.div(row, ratio), lax.rem(row, ratio)

    def other(index, by, size):
        return lax.rem(index + by, size)

    def remote(src, dst, send, recv, target):
        return pltpu.make_async_remote_copy(
            src_ref=src, dst_ref=dst, send_sem=send, recv_sem=recv,
            device_id=target, device_id_type=MESH,
        )

    def column_block(step):
        return lax.rem(step, ratio) * pieces + lax.div(step, ratio)

    def t_copy(j):
        start = pl.multiple_of(j * cw, 128)
        return pltpu.make_async_copy(trans_ref.at[:, pl.ds(start, cw)], tv.at[j], t_sem.at[j])

    def r_copy(step):
        start = pl.multiple_of(column_block(step) * cw, 128)
        slot = lax.rem(step, 2)
        return pltpu.make_async_copy(
            refl_ref.at[:, pl.ds(start, cw)], rbuf.at[slot], r_sem.at[slot]
        )

    def copy_src(c):
        return remote(sall.at[col], sall.at[col], s_send.at[c], s_recv.at[col], (lay, row, c))

    def got_src(c):
        return remote(sall.at[c], sall.at[c], s_send.at[c], s_recv.at[c], (lay, row, c))

    def copy_next(c, p):
        return remote(natd.at[p], nin.at[col, p], n_send.at[c, p], n_recv.at[col, p],
                      (lax.min(lay + 1, last), row, c))

    def got_next(c, p):
        return remote(natd.at[p], nin.at[c, p], n_send.at[c, p], n_recv.at[c, p],
                      (lax.max(lay - 1, 0), row, c))

    def copy_y(c, j):
        return remote(pbuf.at[j, c], ybuf.at[col, j], y_send.at[c, j], y_recv.at[col, j],
                      (lay, row, c))

    def got_y(c, j):
        return remote(pbuf.at[j, c], ybuf.at[c, j], y_send.at[c, j], y_recv.at[c, j],
                      (lay, row, c))

    def copy_z(c, j, own):
        block = pbuf.at[j, col] if own else ybuf.at[c, j]
        goal = ratio * c + lax.div(j, pieces)
        return goal, block, remote(
            block, zbuf.at[row, lax.rem(j, pieces)], z_send.at[c, j],
            z_recv.at[row, lax.rem(j, pieces)], (lay, goal, col),
        )

    def got_z(r, p):
        return remote(natd.at[p], zbuf.at[r, p], z_send.at[0, 0], z_recv.at[r, p],
                      (lay, r, col))

    def copy_g(which, p, r):
        block = (lent, natd, natu)[which].at[p]
        buf, slot = (ginc, 0) if which == 0 else (gup, 1)
        target = (helped, lay, lax.max(lay - 1, 0))[which]
        return block, buf, remote(
            block, buf.at[home_b, p, col], g_send.at[which, p, r],
            g_recv.at[slot, p, home_b, col], (target, r, home_col),
        )

    def got_g(slot, p, b, c):
        buf = gup if slot else ginc
        return remote(natd.at[p], buf.at[b, p, c], g_send.at[0, 0, 0],
                      g_recv.at[slot, p, b, c], (lay, ratio * col + b, c))

    def copy_l(p, target):
        return remote(incn.at[p, col], lent.at[p], l_send.at[p], l_recv.at[p],
                      (target, row, col))

    def send_g(which, p):
        for d in range(1, rows):
            copy_g(which, p, other(row, d, rows))[2].start()
        block, buf, copy = copy_g(which, p, row)
        if which != 1:
            copy.start()
            return

        @pl.when(home_col == col)
        def _():
            buf[home_b, p, col] = block[...]

        @pl.when(home_col != col)
        def _():
            copy.start()

    def sent_g(which, p):
        for d in range(1, rows):
            copy_g(which, p, other(row, d, rows))[2].wait_send()
        copy = copy_g(which, p, row)[2]
        if which != 1:
            copy.wait_send()
            return

        @pl.when(home_col != col)
        def _():
            copy.wait_send()

    def arrived_g(slot, p, b):
        for c in range(cols):
            if slot == 0:
                got_g(slot, p, b, c).wait_recv()
                continue
            mine = (ratio * col + b == row) & (col == c) & (lay == last)

            @pl.when(jnp.logical_not(mine))
            def _():
                got_g(slot, p, b, c).wait_recv()

    def copy_u(c, p):
        return remote(ubuf.at[c, p], urec.at[col, p], u_send.at[c, p], u_recv.at[col, p],
                      (lay, row, c))

    def got_u(c, p):
        return remote(ubuf.at[c, p], urec.at[c, p], u_send.at[c, p], u_recv.at[c, p],
                      (lay, row, c))

    for step in range(chunks):
        t_copy((step % ratio) * pieces + step // ratio).start()

    barrier = pltpu.get_barrier_semaphore()

    def greet(target):
        pl.semaphore_signal(barrier, inc=1, device_id=target, device_id_type=MESH)

    def greet_all(step, carry):
        r, c = lax.div(step, cols), lax.rem(step, cols)
        for d in range(layers):
            l = other(lay, d, layers)
            if d:
                greet((l, r, c))
            else:
                @pl.when((r != row) | (c != col))
                def _():
                    greet((l, r, c))
        return carry

    lax.fori_loop(0, rows * cols, greet_all, 0)
    pl.semaphore_wait(barrier, layers * rows * cols - 1)

    for p in range(pieces):
        sall[col, p] = src_ref[:, p * cw:(p + 1) * cw]
    for d in range(1, cols):
        copy_src(other(col, d, cols)).start()
    for step in range(2):
        r_copy(step).start()
    acc[...] = jnp.zeros_like(acc)
    for d in range(1, cols):
        got_src(other(col, d, cols)).wait_recv()

    def relay():
        for p in range(pieces):
            copy_l(p, helped).wait_recv()
            send_g(0, p)

    @pl.when(lay == 0)
    def _():
        for p in range(pieces):
            incn[p] = sall[:, p]
            copy_l(p, helper).start()

    @pl.when(lay >= half)
    def _():
        relay()

    @pl.when(lay > 0)
    def _():
        for p in range(pieces):
            for c in range(cols):
                got_next(c, p).wait_recv()
            incn[p] = (nin[:, p].astype(F32) + sall[:, p].astype(F32)).astype(BF16)
            copy_l(p, helper).start()

    def to_row(c, j, own):
        goal, block, copy = copy_z(c, j, own)

        @pl.when(goal == row)
        def _():
            zbuf[row, lax.rem(j, pieces)] = block[...]

        @pl.when(goal != row)
        def _():
            copy.start()

    def forward(j):
        for d in range(1, cols):
            c = other(col, d, cols)
            got_y(c, j).wait_recv()
            to_row(c, j, False)

    def down_step(step, carry):
        j = column_block(step)
        t_copy(j).wait()
        total = jnp.zeros((traces, cw), F32)
        for p in range(pieces):
            total += jnp.dot(
                incn[p].reshape(traces, cw), tv[j, pl.ds(p * cw, cw), :],
                preferred_element_type=F32,
            )
        pbuf[j] = total.astype(BF16).reshape(cols, part, cw)
        for d in range(1, cols):
            copy_y(other(col, d, cols), j).start()
        to_row(col, j, True)

        @pl.when(step > 0)
        def _():
            forward(column_block(step - 1))

        return carry

    lax.fori_loop(0, chunks, down_step, 0)
    forward(column_block(chunks - 1))

    for p in range(pieces):
        for d in range(1, rows):
            got_z(other(row, d, rows), p).wait_recv()
        natd[p] = jnp.sum(zbuf[:, p].astype(F32), axis=0).astype(BF16)

        @pl.when(lay < last)
        def _():
            for c in range(cols):
                copy_next(c, p).start()

        @pl.when(lay == last)
        def _():
            send_g(1, p)

    @pl.when(lay < half)
    def _():
        relay()

    contract = (((1,), (1,)), ((), ()))

    def times(lhs, rhs):
        return lax.dot_general(lhs, rhs, contract, preferred_element_type=F32)

    def add_product(lhs, weights):
        for i in range(tiles):
            acc[i] += times(lhs, weights[pl.ds(i * r_tile, r_tile), :])

    def reflect_step(step, carry):
        b, p = lax.rem(step, ratio), lax.div(step, ratio)
        arrived_g(0, p, b)
        r_copy(step).wait()
        add_product(ginc[b, p].reshape(traces, cw), rbuf.at[lax.rem(step, 2)])

        @pl.when(step + 2 < chunks)
        def _():
            r_copy(step + 2).start()

        return carry

    lax.fori_loop(0, chunks, reflect_step, 0)

    def up_step(step, carry):
        b, p = lax.rem(step, ratio), lax.div(step, ratio)
        arrived_g(1, p, b)
        add_product(gup[b, p].reshape(traces, cw), tv.at[b * pieces + p])
        return carry

    lax.fori_loop(0, chunks - ratio, up_step, 0)
    end = pieces - 1
    for b in range(ratio):
        arrived_g(1, end, b)

    per = cw // r_tile

    def piece_of(p, c):
        found = []
        for i in range(per):
            found.append(acc[p * per + i, pl.ds(pl.multiple_of(c * part, 8), part), :])
        return jnp.concatenate(found, axis=1)

    for p in range(pieces):
        for i in range(p * per, (p + 1) * per):
            total = acc[i]
            for b in range(ratio):
                total += times(
                    gup[b, end].reshape(traces, cw),
                    tv[b * pieces + end, pl.ds(i * r_tile, r_tile), :],
                )
            acc[i] = total
        for d in range(1, cols):
            c = other(col, d, cols)
            ubuf[c, p] = piece_of(p, c).astype(BF16)
            copy_u(c, p).start()

    for p in range(pieces):
        total = piece_of(p, col)
        for d in range(1, cols):
            c = other(col, d, cols)
            got_u(c, p).wait_recv()
            total += urec[c, p].astype(F32)
        result = total.astype(BF16)
        natu[p] = result
        out_ref[:, p * cw:(p + 1) * cw] = result

        @pl.when(lay > 0)
        def _():
            send_g(2, p)

    for d in range(1, cols):
        c = other(col, d, cols)
        copy_src(c).wait_send()
        for p in range(pieces):
            copy_u(c, p).wait_send()
        for j in range(chunks):
            copy_y(c, j).wait_send()
    for d in range(cols):
        c = other(col, d, cols)
        for j in range(chunks):
            goal, _, copy = copy_z(c, j, d == 0)

            @pl.when(goal != row)
            def _():
                copy.wait_send()

    for p in range(pieces):
        copy_l(p, helper).wait_send()
        sent_g(0, p)

        @pl.when(lay < last)
        def _():
            for c in range(cols):
                copy_next(c, p).wait_send()

        @pl.when(lay == last)
        def _():
            sent_g(1, p)

        @pl.when(lay > 0)
        def _():
            sent_g(2, p)


def split_of(width):
    for pieces in (4, 3, 2):
        if width % (pieces * 128) == 0:
            return pieces
    return 1


def per_device(layers, rows, cols, sources, transmission, reflection):
    ratio = rows // cols
    own, width = sources.shape[1], sources.shape[2]
    part = -(-own // 16) * 16
    pieces = split_of(width)
    cw = width // pieces
    chunks = ratio * pieces
    r_tile = 256 if cw % 256 == 0 else 128
    traces = cols * part
    src = jnp.pad(sources[0], ((0, part - own), (0, 0)))
    dma, vmem = pltpu.SemaphoreType.DMA, pltpu.VMEM
    result = pl.pallas_call(
        functools.partial(kernel, layers, rows, cols, pieces, r_tile),
        out_shape=jax.ShapeDtypeStruct((part, width), BF16),
        in_specs=[
            pl.BlockSpec(memory_space=pltpu.VMEM),
            pl.BlockSpec(memory_space=pl.ANY),
            pl.BlockSpec(memory_space=pl.ANY),
        ],
        out_specs=pl.BlockSpec(memory_space=pltpu.VMEM),
        scratch_shapes=[
            vmem((chunks, width, cw), BF16),
            vmem((2, width, cw), BF16),
            vmem((cols, pieces, part, cw), BF16),
            vmem((cols, pieces, part, cw), BF16),
            vmem((pieces, cols, part, cw), BF16),
            vmem((chunks, cols, part, cw), BF16),
            vmem((cols, chunks, part, cw), BF16),
            vmem((rows, pieces, part, cw), BF16),
            vmem((pieces, part, cw), BF16),
            vmem((pieces, part, cw), BF16),
            vmem((pieces, part, cw), BF16),
            vmem((ratio, pieces, cols, part, cw), BF16),
            vmem((ratio, pieces, cols, part, cw), BF16),
            vmem((width // r_tile, traces, r_tile), F32),
            vmem((cols, pieces, part, cw), BF16),
            vmem((cols, pieces, part, cw), BF16),
            dma((chunks,)), dma((2,)),
            dma((cols,)), dma((cols,)),
            dma((cols, pieces)), dma((cols, pieces)),
            dma((cols, chunks)), dma((cols, chunks)),
            dma((cols, chunks)), dma((rows, pieces)),
            dma((3, pieces, rows)), dma((2, pieces, ratio, cols)),
            dma((cols, pieces)), dma((cols, pieces)),
            dma((pieces,)), dma((pieces,)),
        ],
        compiler_params=pltpu.CompilerParams(
            collective_id=0, has_side_effects=True, vmem_limit_bytes=66_000_000
        ),
    )(src, transmission[0], reflection[0])
    return result[None, :own]


def solution(mesh):
    sizes = [mesh.shape[name] for name in ("layer", "row", "col")]
    return jax.shard_map(
        functools.partial(per_device, *sizes),
        mesh=mesh,
        in_specs=(P("layer", "col", "row"), P("layer", "row", "col"), P("layer", "row", "col")),
        out_specs=P("layer", "col", "row"),
        check_vma=False,
    )
```

```python
import functools

import jax
import jax.numpy as jnp
from jax import lax
from jax.experimental import pallas as pl
from jax.experimental.pallas import tpu as pltpu
from jax.sharding import PartitionSpec as P

MESH = pl.DeviceIdType.MESH
BF16 = jnp.bfloat16
F32 = jnp.float32


def kernel(
    layers, rows, cols, pieces, r_tile,
    src_ref, trans_ref, refl_ref, out_ref,
    tv, rbuf, sall, nin, incn, pbuf, ybuf, zbuf, natd, natu, lent, ginc, gup, acc, ubuf, urec,
    t_sem, r_sem, s_send, s_recv, n_send, n_recv, y_send, y_recv, z_send, z_recv,
    g_send, g_recv, u_send, u_recv, l_send, l_recv,
):
    ratio = rows // cols
    chunks = ratio * pieces
    lay, row, col = (lax.axis_index(name) for name in ("layer", "row", "col"))
    part, cw = natd.shape[1], natd.shape[2]
    traces = cols * part
    tiles = acc.shape[0]
    last = layers - 1
    half = layers // 2
    helper = lax.rem(lay + half, layers)
    helped = lax.rem(lay + layers - half, layers)
    home_col, home_b = lax.div(row, ratio), lax.rem(row, ratio)

    def other(index, by, size):
        return lax.rem(index + by, size)

    def remote(src, dst, send, recv, target):
        return pltpu.make_async_remote_copy(
            src_ref=src, dst_ref=dst, send_sem=send, recv_sem=recv,
            device_id=target, device_id_type=MESH,
        )

    def column_block(step):
        return lax.rem(step, ratio) * pieces + lax.div(step, ratio)

    def t_copy(j):
        start = pl.multiple_of(j * cw, 128)
        return pltpu.make_async_copy(trans_ref.at[:, pl.ds(start, cw)], tv.at[j], t_sem.at[j])

    def r_copy(step):
        start = pl.multiple_of(column_block(step) * cw, 128)
        slot = lax.rem(step, 2)
        return pltpu.make_async_copy(
            refl_ref.at[:, pl.ds(start, cw)], rbuf.at[slot], r_sem.at[slot]
        )

    def copy_src(c):
        return remote(sall.at[col], sall.at[col], s_send.at[c], s_recv.at[col], (lay, row, c))

    def got_src(c):
        return remote(sall.at[c], sall.at[c], s_send.at[c], s_recv.at[c], (lay, row, c))

    def copy_next(c, p):
        return remote(natd.at[p], nin.at[col, p], n_send.at[c, p], n_recv.at[col, p],
                      (lax.min(lay + 1, last), row, c))

    def got_next(c, p):
        return remote(natd.at[p], nin.at[c, p], n_send.at[c, p], n_recv.at[c, p],
                      (lax.max(lay - 1, 0), row, c))

    def copy_y(c, j):
        return remote(pbuf.at[j, c], ybuf.at[col, j], y_send.at[c, j], y_recv.at[col, j],
                      (lay, row, c))

    def got_y(c, j):
        return remote(pbuf.at[j, c], ybuf.at[c, j], y_send.at[c, j], y_recv.at[c, j],
                      (lay, row, c))

    def copy_z(c, j, own):
        block = pbuf.at[j, col] if own else ybuf.at[c, j]
        goal = ratio * c + lax.div(j, pieces)
        return goal, block, remote(
            block, zbuf.at[row, lax.rem(j, pieces)], z_send.at[c, j],
            z_recv.at[row, lax.rem(j, pieces)], (lay, goal, col),
        )

    def got_z(r, p):
        return remote(natd.at[p], zbuf.at[r, p], z_send.at[0, 0], z_recv.at[r, p],
                      (lay, r, col))

    def copy_g(which, p, r):
        block = (lent, natd, natu)[which].at[p]
        buf, slot = (ginc, 0) if which == 0 else (gup, 1)
        target = (helped, lay, lax.max(lay - 1, 0))[which]
        return block, buf, remote(
            block, buf.at[home_b, p, col], g_send.at[which, p, r],
            g_recv.at[slot, p, home_b, col], (target, r, home_col),
        )

    def got_g(slot, p, b, c):
        buf = gup if slot else ginc
        return remote(natd.at[p], buf.at[b, p, c], g_send.at[0, 0, 0],
                      g_recv.at[slot, p, b, c], (lay, ratio * col + b, c))

    def copy_l(p, target):
        return remote(incn.at[p, col], lent.at[p], l_send.at[p], l_recv.at[p],
                      (target, row, col))

    def send_g(which, p):
        for d in range(1, rows):
            copy_g(which, p, other(row, d, rows))[2].start()
        block, buf, copy = copy_g(which, p, row)
        if which != 1:
            copy.start()
            return

        @pl.when(home_col == col)
        def _():
            buf[home_b, p, col] = block[...]

        @pl.when(home_col != col)
        def _():
            copy.start()

    def sent_g(which, p):
        for d in range(1, rows):
            copy_g(which, p, other(row, d, rows))[2].wait_send()
        copy = copy_g(which, p, row)[2]
        if which != 1:
            copy.wait_send()
            return

        @pl.when(home_col != col)
        def _():
            copy.wait_send()

    def arrived_g(slot, p, b):
        for c in range(cols):
            if slot == 0:
                got_g(slot, p, b, c).wait_recv()
                continue
            mine = (ratio * col + b == row) & (col == c) & (lay == last)

            @pl.when(jnp.logical_not(mine))
            def _():
                got_g(slot, p, b, c).wait_recv()

    def copy_u(c, p):
        return remote(ubuf.at[c, p], urec.at[col, p], u_send.at[c, p], u_recv.at[col, p],
                      (lay, row, c))

    def got_u(c, p):
        return remote(ubuf.at[c, p], urec.at[c, p], u_send.at[c, p], u_recv.at[c, p],
                      (lay, row, c))

    for step in range(chunks):
        t_copy((step % ratio) * pieces + step // ratio).start()

    barrier = pltpu.get_barrier_semaphore()

    def greet(target):
        pl.semaphore_signal(barrier, inc=1, device_id=target, device_id_type=MESH)

    def greet_all(step, carry):
        r, c = lax.div(step, cols), lax.rem(step, cols)
        for d in range(layers):
            l = other(lay, d, layers)
            if d:
                greet((l, r, c))
            else:
                @pl.when((r != row) | (c != col))
                def _():
                    greet((l, r, c))
        return carry

    lax.fori_loop(0, rows * cols, greet_all, 0)
    pl.semaphore_wait(barrier, layers * rows * cols - 1)

    for p in range(pieces):
        sall[col, p] = src_ref[:, p * cw:(p + 1) * cw]
    for d in range(1, cols):
        copy_src(other(col, d, cols)).start()
    acc[...] = jnp.zeros_like(acc)
    for d in range(1, cols):
        got_src(other(col, d, cols)).wait_recv()

    def relay():
        for p in range(pieces):
            copy_l(p, helped).wait_recv()
            send_g(0, p)

    @pl.when(lay == 0)
    def _():
        for p in range(pieces):
            incn[p] = sall[:, p]

    @pl.when(lay >= half)
    def _():
        relay()

    @pl.when(lay > 0)
    def _():
        for p in range(pieces):
            for c in range(cols):
                got_next(c, p).wait_recv()
            incn[p] = (nin[:, p].astype(F32) + sall[:, p].astype(F32)).astype(BF16)

    def to_row(c, j, own):
        goal, block, copy = copy_z(c, j, own)

        @pl.when(goal == row)
        def _():
            zbuf[row, lax.rem(j, pieces)] = block[...]

        @pl.when(goal != row)
        def _():
            copy.start()

    def forward(j):
        for d in range(1, cols):
            c = other(col, d, cols)
            got_y(c, j).wait_recv()
            to_row(c, j, False)

    def down_step(step, carry):
        j = column_block(step)
        t_copy(j).wait()
        total = jnp.zeros((traces, cw), F32)
        for p in range(pieces):
            total += jnp.dot(
                incn[p].reshape(traces, cw), tv[j, pl.ds(p * cw, cw), :],
                preferred_element_type=F32,
            )
        pbuf[j] = total.astype(BF16).reshape(cols, part, cw)
        for d in range(1, cols):
            copy_y(other(col, d, cols), j).start()
        to_row(col, j, True)

        @pl.when(step > 0)
        def _():
            forward(column_block(step - 1))

        return carry

    lax.fori_loop(0, chunks, down_step, 0)
    forward(column_block(chunks - 1))
    for p in range(pieces):
        copy_l(p, helper).start()
    for step in range(2):
        r_copy(step).start()

    for p in range(pieces):
        for d in range(1, rows):
            got_z(other(row, d, rows), p).wait_recv()
        natd[p] = jnp.sum(zbuf[:, p].astype(F32), axis=0).astype(BF16)

        @pl.when(lay < last)
        def _():
            for c in range(cols):
                copy_next(c, p).start()

        @pl.when(lay == last)
        def _():
            send_g(1, p)

    @pl.when(lay < half)
    def _():
        relay()

    contract = (((1,), (1,)), ((), ()))

    def times(lhs, rhs):
        return lax.dot_general(lhs, rhs, contract, preferred_element_type=F32)

    def add_product(lhs, weights):
        for i in range(tiles):
            acc[i] += times(lhs, weights[pl.ds(i * r_tile, r_tile), :])

    def reflect_step(step, carry):
        b, p = lax.rem(step, ratio), lax.div(step, ratio)
        arrived_g(0, p, b)
        r_copy(step).wait()
        add_product(ginc[b, p].reshape(traces, cw), rbuf.at[lax.rem(step, 2)])

        @pl.when(step + 2 < chunks)
        def _():
            r_copy(step + 2).start()

        return carry

    lax.fori_loop(0, chunks, reflect_step, 0)

    def up_step(step, carry):
        b, p = lax.rem(step, ratio), lax.div(step, ratio)
        arrived_g(1, p, b)
        add_product(gup[b, p].reshape(traces, cw), tv.at[b * pieces + p])
        return carry

    lax.fori_loop(0, chunks - ratio, up_step, 0)
    end = pieces - 1
    for b in range(ratio):
        arrived_g(1, end, b)

    per = cw // r_tile

    def piece_of(p, c):
        found = []
        for i in range(per):
            found.append(acc[p * per + i, pl.ds(pl.multiple_of(c * part, 8), part), :])
        return jnp.concatenate(found, axis=1)

    for p in range(pieces):
        for i in range(p * per, (p + 1) * per):
            total = acc[i]
            for b in range(ratio):
                total += times(
                    gup[b, end].reshape(traces, cw),
                    tv[b * pieces + end, pl.ds(i * r_tile, r_tile), :],
                )
            acc[i] = total
        for d in range(1, cols):
            c = other(col, d, cols)
            ubuf[c, p] = piece_of(p, c).astype(BF16)
            copy_u(c, p).start()

    for p in range(pieces):
        total = piece_of(p, col)
        for d in range(1, cols):
            c = other(col, d, cols)
            got_u(c, p).wait_recv()
            total += urec[c, p].astype(F32)
        result = total.astype(BF16)
        natu[p] = result
        out_ref[:, p * cw:(p + 1) * cw] = result

        @pl.when(lay > 0)
        def _():
            send_g(2, p)

    for d in range(1, cols):
        c = other(col, d, cols)
        copy_src(c).wait_send()
        for p in range(pieces):
            copy_u(c, p).wait_send()
        for j in range(chunks):
            copy_y(c, j).wait_send()
    for d in range(cols):
        c = other(col, d, cols)
        for j in range(chunks):
            goal, _, copy = copy_z(c, j, d == 0)

            @pl.when(goal != row)
            def _():
                copy.wait_send()

    for p in range(pieces):
        copy_l(p, helper).wait_send()
        sent_g(0, p)

        @pl.when(lay < last)
        def _():
            for c in range(cols):
                copy_next(c, p).wait_send()

        @pl.when(lay == last)
        def _():
            sent_g(1, p)

        @pl.when(lay > 0)
        def _():
            sent_g(2, p)


def split_of(width):
    for pieces in (4, 3, 2):
        if width % (pieces * 128) == 0:
            return pieces
    return 1


def per_device(layers, rows, cols, sources, transmission, reflection):
    ratio = rows // cols
    own, width = sources.shape[1], sources.shape[2]
    part = -(-own // 16) * 16
    pieces = split_of(width)
    cw = width // pieces
    chunks = ratio * pieces
    r_tile = 256 if cw % 256 == 0 else 128
    traces = cols * part
    src = jnp.pad(sources[0], ((0, part - own), (0, 0)))
    dma, vmem = pltpu.SemaphoreType.DMA, pltpu.VMEM
    result = pl.pallas_call(
        functools.partial(kernel, layers, rows, cols, pieces, r_tile),
        out_shape=jax.ShapeDtypeStruct((part, width), BF16),
        in_specs=[
            pl.BlockSpec(memory_space=pltpu.VMEM),
            pl.BlockSpec(memory_space=pl.ANY),
            pl.BlockSpec(memory_space=pl.ANY),
        ],
        out_specs=pl.BlockSpec(memory_space=pltpu.VMEM),
        scratch_shapes=[
            vmem((chunks, width, cw), BF16),
            vmem((2, width, cw), BF16),
            vmem((cols, pieces, part, cw), BF16),
            vmem((cols, pieces, part, cw), BF16),
            vmem((pieces, cols, part, cw), BF16),
            vmem((chunks, cols, part, cw), BF16),
            vmem((cols, chunks, part, cw), BF16),
            vmem((rows, pieces, part, cw), BF16),
            vmem((pieces, part, cw), BF16),
            vmem((pieces, part, cw), BF16),
            vmem((pieces, part, cw), BF16),
            vmem((ratio, pieces, cols, part, cw), BF16),
            vmem((ratio, pieces, cols, part, cw), BF16),
            vmem((width // r_tile, traces, r_tile), F32),
            vmem((cols, pieces, part, cw), BF16),
            vmem((cols, pieces, part, cw), BF16),
            dma((chunks,)), dma((2,)),
            dma((cols,)), dma((cols,)),
            dma((cols, pieces)), dma((cols, pieces)),
            dma((cols, chunks)), dma((cols, chunks)),
            dma((cols, chunks)), dma((rows, pieces)),
            dma((3, pieces, rows)), dma((2, pieces, ratio, cols)),
            dma((cols, pieces)), dma((cols, pieces)),
            dma((pieces,)), dma((pieces,)),
        ],
        compiler_params=pltpu.CompilerParams(
            collective_id=0, has_side_effects=True, vmem_limit_bytes=66_000_000
        ),
    )(src, transmission[0], reflection[0])
    return result[None, :own]


def solution(mesh):
    sizes = [mesh.shape[name] for name in ("layer", "row", "col")]
    return jax.shard_map(
        functools.partial(per_device, *sizes),
        mesh=mesh,
        in_specs=(P("layer", "col", "row"), P("layer", "row", "col"), P("layer", "row", "col")),
        out_specs=P("layer", "col", "row"),
        check_vma=False,
    )
```
